32 devices in a mesh: grp: 8 (over z, x), lane: 4 (over y, core).
Axes of the slice: x: 2, y: 2, z: 4, core: 2. Of those that a mesh axis runs over, the one named last changes fastest.
Arguments:
- features: bfloat16 [65536, 128], P(('grp', 'lane')), may hold values from -600 to 600
- tiles: bfloat16 [512, 7, 128, 128], P(('grp', 'lane')), may hold values from -0.125 to 0.125
- tile_cols: int32 [512, 7], P(('grp', 'lane')), may hold values from 0 to 23
- send_index: int32 [32, 2, 512], P(('grp', 'lane')), may hold values from 0 to 2047
- send_count: int32 [32, 2], P(('grp', 'lane')), may hold values from 128 to 512, as said below
- coef: float32 [4, 128], replicated, may hold values from -1 to 1
- dest_lane: int32 [65536], P(('grp', 'lane')), may hold values from 0 to 3, as said below
- dest_slot: int32 [65536], P(('grp', 'lane')), may hold values from 0 to 2047, as said below
Outputs:
- table_out: bfloat16 [65536, 128], P(('grp', 'lane'))
The draws below stay inside these ranges and needn't reach their ends.
Inputs may be any that keep to these rules, and one draw needn't show every extreme that they name: `send_count`: in every draw for each of the two directions some partition has exactly 512 live rows towards that neighbour. `dest_lane`: within each relayout group every row of every table shard is named by exactly one node; at most 1024 rows of one partition go to one shard, and exactly 1024 for some pair in every group. `dest_slot`: together with dest_lane, a one-to-one map of a group's nodes onto its table rows.
All inputs are finite; a program needn't handle non-finite values.
Results may differ from the reference program's by a relative error of at most 0.008.
Values may be sent and summed in bfloat16 or wider, within the bound.
A program may use at most 64 MiB of HBM per device.

```python
import math
import jax
import jax.numpy as jnp
from jax import lax

F = 128
TILE = 128
KT = 7
ORDER = 3
ROWS = 2048
BND = 512
NODES = 65536
N_GRP = 8
N_LANE = 4
DEVICES = 32


def draw_features(key, part):
    first_key, second_key, third_key = jax.random.split(key, 3)
    position = jnp.arange(NODES).astype(jnp.float32)[:, None] / NODES
    row_scale = jnp.exp(jax.random.uniform(second_key, (NODES, 1)) * math.log(10.0))
    col_scale = jnp.exp(jax.random.uniform(third_key, (1, F)) * math.log(10.0))
    values = jnp.clip(jax.random.normal(first_key, (NODES, F)), -6.0, 6.0)
    ramp = 1.0 + 2.0 * position
    return (values * row_scale * col_scale * ramp / 10.0).astype(jnp.bfloat16)


def draw_send_count(key, part):
    first_key, second_key = jax.random.split(jax.random.fold_in(key, 11), 2)
    counts = jax.random.randint(first_key, (DEVICES, 2), BND // 4, BND + 1)
    fullest = jax.random.randint(second_key, (2,), 0, DEVICES)
    counts = counts.at[fullest[0], 0].set(BND)
    counts = counts.at[fullest[1], 1].set(BND)
    return counts.astype(jnp.int32)


def relay_plan(key):
    base_key = jax.random.fold_in(key, 77)
    mean_load = ROWS // N_LANE
    lane_ids = jnp.arange(N_LANE)
    lane_load = jnp.where(lane_ids == 0, 2 * mean_load, jnp.where((lane_ids == 1) | (lane_ids == 2), mean_load // 2, mean_load))
    rotation = jax.random.randint(jax.random.fold_in(base_key, 1), (N_GRP,), 0, N_LANE)
    counts = lane_load[(lane_ids[None, None, :] - lane_ids[None, :, None] + rotation[:, None, None]) % N_LANE]
    run_ends = jnp.cumsum(counts, axis=2)
    run_starts = run_ends - counts
    position = jnp.arange(ROWS)
    sorted_dest = jnp.sum((position[None, None, :, None] >= run_ends[:, :, None, :]).astype(jnp.int32), axis=3)
    rank_in_run = position[None, None, :] - jnp.take_along_axis(run_starts, sorted_dest, axis=2)
    offsets = jnp.cumsum(counts, axis=1) - counts
    placement = jnp.take_along_axis(offsets, sorted_dest, axis=2) + rank_in_run
    row_keys = jax.random.split(jax.random.fold_in(base_key, 2), N_GRP * N_LANE)
    shuffle = jax.vmap(lambda k: jax.random.permutation(k, ROWS))(row_keys).reshape(N_GRP, N_LANE, ROWS)
    destination = jnp.take_along_axis(sorted_dest, shuffle, axis=2)
    place_rows = jnp.take_along_axis(placement, shuffle, axis=2)
    slot_keys = jax.random.split(jax.random.fold_in(base_key, 3), N_GRP * N_LANE)
    slot_perm = jax.vmap(lambda k: jax.random.permutation(k, ROWS))(slot_keys).reshape(N_GRP, N_LANE, ROWS)
    group_ids = jnp.arange(N_GRP)[:, None, None]
    slot_ids = slot_perm[group_ids, destination, place_rows]
    return (destination.reshape(-1).astype(jnp.int32), slot_ids.reshape(-1).astype(jnp.int32))


def draw_dest_lane(key, part):
    return relay_plan(key)[0]


def draw_dest_slot(key, part):
    return relay_plan(key)[1]


def plant(array, stream_key, low, high):
    longest = array.shape.index(max(array.shape))
    spots = []
    for shift in (0, 1):
        where = [jax.random.randint(jax.random.fold_in(stream_key, axis), (), 0, length) for axis, length in enumerate(array.shape)]
        where[longest] = (where[longest] + shift) % array.shape[longest]
        spots.append(tuple(where))
    return array.at[spots[0]].set(low).at[spots[1]].set(high)


def block_scale(stream_key, extent, shards, least, top_value):
    level, own = 1.0, jax.random.fold_in(stream_key, 6)
    for dim, blocks in shards:
        heights = jnp.exp(jax.random.uniform(jax.random.fold_in(own, dim), (blocks,), jnp.float32, least / len(shards), top_value / len(shards)))
        level = level * jnp.repeat(heights, extent[dim] // blocks).reshape([-1 if axis == dim else 1 for axis in range(len(extent))])
    return level


def centred(own_key, dims, scale, bound, pieces=(), dtype=jnp.bfloat16):
    array = jax.random.normal(own_key, dims, jnp.float32) * scale
    if len(pieces) > 0:
        array = block_scale(own_key, dims, pieces, -0.22, 0.18) * array
    return jnp.clip(array, min=-bound, max=bound).astype(dtype)


def setup_inputs(seed: int = 0) -> dict:
    keys = jax.random.split(jax.random.key(seed), 9)
    features = draw_features(jax.random.fold_in(keys[8], 71), 0)
    tiles = centred(keys[1], (NODES // TILE, KT, TILE, TILE), (2 * KT * TILE) ** -0.5, 0.125, ((0, 32),))
    tile_cols = plant(jax.random.randint(keys[2], (NODES // TILE, KT), 0, ROWS // TILE + 2 * BND // TILE), jax.random.fold_in(keys[2], 1), 0, (ROWS // TILE + 2 * BND // TILE) - 1).astype(jnp.int32)
    send_index = plant(jax.random.randint(keys[3], (DEVICES, 2, BND), 0, ROWS), jax.random.fold_in(keys[3], 1), 0, ROWS - 1).astype(jnp.int32)
    send_count = draw_send_count(jax.random.fold_in(keys[8], 71), 0)
    coef = jnp.clip(jax.random.uniform(keys[5], (ORDER + 1, F), jnp.float32, -1.0, 1.0), -1.0, 1.0)
    dest_lane = draw_dest_lane(jax.random.fold_in(keys[8], 71), 0)
    dest_slot = draw_dest_slot(jax.random.fold_in(keys[8], 71), 0)
    return {"features": features, "tiles": tiles, "tile_cols": tile_cols, "send_index": send_index, "send_count": send_count, "coef": coef, "dest_lane": dest_lane, "dest_slot": dest_slot}


def operate_all(current, tile_set, column_ids, index_set, valid_rows):
    picked = jax.vmap(jax.vmap(lambda c, i: c[i]))(current, index_set)
    picked = jnp.where(valid_rows[..., None], picked, jnp.zeros_like(picked))
    from_lower = jnp.roll(picked[:, :, 0], 1, axis=0)
    from_upper = jnp.roll(picked[:, :, 1], -1, axis=0)
    extended = jnp.concatenate([current, from_lower, from_upper], axis=2)
    extended = extended.reshape(N_GRP, N_LANE, -1, TILE, F)

    def per_group(packed):
        group_ext, group_tiles, group_cols = packed

        def per_device(dev_ext, dev_tiles, dev_cols):
            blocks = dev_ext[dev_cols].astype(jnp.float32)
            result = jnp.einsum('bkij,bkjf->bif', dev_tiles.astype(jnp.float32), blocks)
            return result.reshape(ROWS, F)
        return jax.vmap(per_device)(group_ext, group_tiles, group_cols)
    return lax.map(per_group, (extended, tile_set, column_ids))

def reference(features, tiles, tile_cols, send_index, send_count, coef, dest_lane, dest_slot):
    blocks_dev = ROWS // TILE
    tile_set = tiles.reshape(N_GRP, N_LANE, blocks_dev, KT, TILE, TILE)
    column_ids = tile_cols.reshape(N_GRP, N_LANE, blocks_dev, KT)
    index_set = send_index.reshape(N_GRP, N_LANE, 2, BND)
    counts = send_count.reshape(N_GRP, N_LANE, 2)
    valid_rows = jnp.arange(BND).astype(jnp.int32)[None, None, None, :] < counts[..., None]
    cheb_terms = [features.reshape(N_GRP, N_LANE, ROWS, F)]
    first = operate_all(cheb_terms[0], tile_set, column_ids, index_set, valid_rows)
    cheb_terms.append(first.astype(jnp.bfloat16))
    for term_order in range(2, ORDER + 1):
        applied = operate_all(cheb_terms[-1], tile_set, column_ids, index_set, valid_rows)
        nxt = 2.0 * applied - cheb_terms[-2].astype(jnp.float32)
        cheb_terms.append(nxt.astype(jnp.bfloat16))
    mixed = jnp.zeros((NODES, F), jnp.float32)
    for term_order in range(ORDER + 1):
        mixed = mixed + coef[term_order][None, :] * cheb_terms[term_order].reshape(NODES, F).astype(jnp.float32)
    gram = jnp.dot(mixed.T, mixed, precision=lax.Precision.HIGHEST)
    factor = jnp.linalg.cholesky(gram)
    white = jax.scipy.linalg.solve_triangular(factor, mixed.T, lower=True).T * jnp.sqrt(jnp.float32(NODES))
    norms = jnp.sqrt(lax.optimization_barrier(jnp.sum(white * white, axis=1, keepdims=True)) + 1e-06)
    radius = jnp.sqrt(jnp.float32(F))
    ball_rows = (jnp.tanh(norms / radius) * radius * white / norms).astype(jnp.bfloat16)
    group_of = jnp.arange(NODES).astype(jnp.int32) // (N_LANE * ROWS)
    target = (group_of * N_LANE + dest_lane) * ROWS + dest_slot
    table_out = jnp.zeros((NODES, F), jnp.bfloat16).at[target].set(ball_rows)
    return table_out
```

```python
import functools
import math

import jax
import jax.numpy as jnp
from jax import lax
from jax.experimental import pallas as pl
from jax.experimental.pallas import tpu as pltpu
from jax.sharding import PartitionSpec as P

MESH = pl.DeviceIdType.MESH
BF = jnp.bfloat16
F32 = jnp.float32
ORDER = 3
SUB = 8
PIVOTS = 16


def onehot(flags):
    return jnp.where(flags, 1.0, 0.0).astype(BF)


def splat(rows, at, axis):
    return jnp.broadcast_to(lax.slice_in_dim(rows, at, at + 1, axis=axis), (SUB, rows.shape[1]))


def eliminate(gram, node_total):
    size = gram.shape[0]
    parts = PIVOTS // SUB
    root = math.sqrt(node_total)
    lane = lax.broadcasted_iota(jnp.int32, (SUB, size), 1)
    sub = lax.broadcasted_iota(jnp.int32, (SUB, size), 0)
    state = gram
    result = []
    for first in range(0, size, PIVOTS):
        last = first + PIVOTS
        block = [state[first + SUB * v : first + SUB * (v + 1), :] for v in range(parts)]
        cols = [[splat(block[v], first + q, 1) for v in range(parts)] for q in range(PIVOTS)]
        rows = [jnp.zeros((SUB, size), F32) for _ in range(parts)]
        for r in range(PIVOTS):
            own, row = divmod(r, SUB)
            here = lane == first + r
            col = cols[r]
            pivot = splat(col[own], row, 0)
            inverse = 1.0 / pivot
            pivot_row = splat(block[own], row, 0)
            forward = jnp.where(here, 1.0, jnp.where(lane < first + r, pivot_row, 0.0))
            rows[own] = jnp.where(sub == row, forward * (root * lax.rsqrt(pivot)), rows[own])
            scaled = jnp.where(here, 1.0, pivot_row) * inverse
            for v in range(parts):
                kept = jnp.where(here, 0.0, block[v]) - col[v] * scaled
                block[v] = jnp.where(sub == row, scaled, kept) if v == own else kept
            for q in range(r + 1, PIVOTS):
                factor = splat(cols[q][own], row, 0) * inverse
                for v in range(parts):
                    kept = cols[q][v] - col[v] * factor
                    cols[q][v] = jnp.where(sub == row, factor, kept) if v == own else kept
        result += rows
        if last < size:
            rest = state[last:, :]
            pad = [jnp.zeros((size - last, size), F32)]
            if first:
                pad = [jnp.zeros((first, size), F32)] + block + pad
            else:
                pad = block + pad
            update = jnp.dot(
                rest, jnp.concatenate(pad, axis=0), precision=lax.Precision.HIGHEST, preferred_element_type=F32
            )
            at = lax.broadcasted_iota(jnp.int32, rest.shape, 1)
            rest = jnp.where((at >= first) & (at < last), 0.0, rest) - update
            state = jnp.concatenate([state[:last], rest], axis=0)
    return jnp.concatenate(result, axis=0)


def kernel(
    groups, lanes, cols_h, counts_h, feats, tiles, index_h, coef_h, dest_lane_h, dest_slot_h, out,
    cols, counts, index, coef, dest_lane, dest_slot, source_v, source_s,
    ext0, ext1, ext2, tile_v, pick, snd, mixed, low, gat, codes, part, rs_buf, lane_buf, chunk, tot, wide,
    load_sem, halo_s, halo_r, code_s, code_r, rs_s, rs_r, ln_s, ln_r, ag_s, ag_r, x_s, x_r, f_s, f_r,
):
    g, l = lax.axis_index("grp"), lax.axis_index("lane")
    own_blocks, tile, width = feats.shape
    rows = own_blocks * tile
    ext = (ext0, ext1, ext2)
    per_block = tiles.shape[1]
    bnd = index_h.shape[1]
    lists = bnd // tile
    node_total = rows * groups * lanes
    half = lanes // 2
    sibling = l + 1 - 2 * lax.rem(l, 2)

    def grp_at(t):
        return (lax.rem(g + t + groups, groups), l)

    def lane_at(t):
        return (g, lax.rem(l + t + lanes, lanes))

    load_tiles = pltpu.make_async_copy(tiles, tile_v, load_sem.at[0])
    load_feats = pltpu.make_async_copy(feats, ext[0].at[pl.ds(0, own_blocks)], load_sem.at[1])
    small = [
        pltpu.make_async_copy(src, dst, load_sem.at[2 + i])
        for i, (src, dst) in enumerate(
            [
                (index_h, index), (counts_h, counts), (dest_lane_h, dest_lane),
                (dest_slot_h, dest_slot), (cols_h, cols), (coef_h, coef),
            ]
        )
    ]
    for copy in small[:4]:
        copy.start()
    load_feats.start()
    load_tiles.start()
    for copy in small[4:]:
        copy.start()

    barrier = pltpu.get_barrier_semaphore()
    for t in range(1, groups):
        pl.semaphore_signal(barrier, inc=1, device_id=grp_at(t), device_id_type=MESH)
    for t in range(1, lanes):
        pl.semaphore_signal(barrier, inc=1, device_id=lane_at(t), device_id_type=MESH)

    for copy in small[:4]:
        copy.wait()
    codes[0] = dest_lane[...] * rows + dest_slot[...]

    row_pos = lax.broadcasted_iota(jnp.int32, (tile, tile), 0)
    lane_pos = lax.broadcasted_iota(jnp.int32, (tile, tile), 1)
    for d in range(2):
        for c in range(bnd // tile):
            wanted = jnp.broadcast_to(index[d : d + 1, c * tile : (c + 1) * tile], (tile, tile)).T
            wanted = jnp.where(row_pos + c * tile < counts[0, d], wanted, -1)
            for r in range(rows // tile):
                pick[pl.ds(d * bnd + c * tile, tile), pl.ds(r * tile, tile)] = onehot(
                    wanted == lane_pos + r * tile
                )

    load_feats.wait()
    pl.semaphore_wait(barrier, groups - 1 + lanes - 1)

    def remote(src, dst, s, r, device):
        return pltpu.make_async_remote_copy(
            src_ref=src, dst_ref=dst, send_sem=s, recv_sem=r, device_id=device, device_id_type=MESH
        )

    def halo(k):
        copies = []
        for d in range(2):
            def gather(c, _, d=d):
                at = pl.multiple_of(d * bnd + c * 256, 256)
                picked = jnp.dot(
                    pick[pl.ds(at, 256), :], ext[k][pl.ds(0, own_blocks)].reshape(rows, width),
                    preferred_element_type=F32
                ).astype(BF)
                for part_at in range(256 // tile):
                    snd[k, (d * bnd + c * 256) // tile + part_at] = picked[
                        part_at * tile : (part_at + 1) * tile
                    ]
                return 0
            lax.fori_loop(0, bnd // 256, gather, 0)
            copy = remote(
                snd.at[k, pl.ds(d * lists, lists)], ext[k].at[pl.ds(own_blocks + d * lists, lists)],
                halo_s.at[k, d], halo_r.at[k, d], grp_at(1 - 2 * d),
            )
            copy.start()
            copies.append(copy)
        return copies

    def invert():
        found = jnp.zeros((2 * own_blocks, tile), F32)
        high_pos = lax.broadcasted_iota(jnp.int32, (own_blocks, tile), 0)
        low_pos = lax.broadcasted_iota(jnp.int32, (own_blocks, tile), 1).astype(F32)
        for s in range(lanes):
            code = codes[passed_code(s - half) if s >= half else 2 * s] - l * rows
            left, right = [], []
            for r in range(own_blocks):
                one = code[r : r + 1, :]
                hit = jnp.where(one // tile == high_pos, 1.0, 0.0)
                left.append(
                    jnp.concatenate([hit * float(s * own_blocks + r), hit * low_pos], axis=0).astype(BF)
                )
                right.append(onehot(row_pos == jnp.bitwise_and(one, tile - 1)))
            found = found + lax.dot_general(
                jnp.concatenate(left, axis=1), jnp.concatenate(right, axis=1),
                (((1,), (1,)), ((), ())), preferred_element_type=F32,
            )
        source = found[:own_blocks] * float(tile) + found[own_blocks:]
        source_v[...] = jnp.clip(source.astype(jnp.int32), 0, lanes * rows - 1)
        copy = pltpu.make_async_copy(source_v, source_s, load_sem.at[0])
        copy.start()
        return copy

    def widen(slot):
        def step(c, _):
            at = pl.multiple_of(c * 256, 256)
            wide[pl.ds(slot * rows + at, 256)] = gat[slot, pl.ds(at, 256)].astype(F32)
            return 0

        lax.fori_loop(0, rows // 256, step, 0, unroll=2)

    def passed_code(t):
        return lax.rem(l - sibling + 2 * t + lanes, lanes)

    halo_copies = halo(0)
    code_copies = []
    for t in range(1, lanes):
        copy = remote(codes.at[0], codes.at[t], code_s.at[t], code_r.at[t], lane_at(t))
        copy.start()
        code_copies.append(copy)
    load_tiles.wait()
    for copy in small[4:]:
        copy.wait()

    for k in range(1, ORDER + 1):
        for copy in halo_copies:
            copy.wait()

        def block(b, _, k=k):
            at = pl.ds(pl.multiple_of(b * tile, tile), tile)
            lhs = jnp.concatenate([tile_v[b, j] for j in range(per_block)], axis=1)
            rhs = jnp.concatenate(
                [
                    ext[k - 1][cols[j, b]]
                    for j in range(per_block)
                ],
                axis=0,
            )
            value = jnp.dot(lhs, rhs, preferred_element_type=F32)
            if k > 1:
                value = 2.0 * value - ext[k - 2][b].astype(F32)
            term = value.astype(BF)
            if k == 1:
                total = coef[0:1, :] * ext[0][b].astype(F32)
            else:
                total = mixed[at]
            total = total + coef[k : k + 1, :] * term.astype(F32)
            if k < ORDER:
                ext[k][b] = term
                mixed[at] = total
            else:
                high = total.astype(BF)
                gat[0, at] = high
                low[at] = (total - high.astype(F32)).astype(BF)
            return 0

        lax.fori_loop(0, rows // tile, block, 0, unroll=16)
        if k < ORDER:
            halo_copies = halo(k)
            if k == 1:
                for copy in code_copies:
                    copy.wait()
                source_copy = invert()

    step = 512
    square = jnp.zeros((2 * width, 2 * width), F32)
    for c in range(rows // step):
        both = jnp.concatenate([gat[0, pl.ds(c * step, step)], low[pl.ds(c * step, step)]], axis=1)
        square = square + lax.dot_general(
            both, both, (((0,), (0,)), ((), ())), preferred_element_type=F32
        )
    own_gram = (square[:width, :width] + square[width:, width:]) + (
        square[:width, width:] + square[width:, :width]
    )
    share = width // groups
    for t in range(groups):
        part[t] = own_gram[t * share : (t + 1) * share, :]

    rs_copies = []
    for t in range(1, groups):
        peer = grp_at(t)
        copy = remote(part.at[peer[0]], rs_buf.at[t], rs_s.at[t], rs_r.at[t], peer)
        copy.start()
        rs_copies.append(copy)
    sib_copies = [remote(gat.at[0], gat.at[half], f_s.at[0], f_r.at[0], (g, sibling))]
    sib_copies[0].start()
    widen(0)

    for copy in rs_copies:
        copy.wait()
    summed = part[g]
    for t in range(1, groups):
        summed = summed + rs_buf[t]
    lane_buf[0] = summed
    ln_copies = []
    for t in range(1, lanes):
        copy = remote(lane_buf.at[0], lane_buf.at[t], ln_s.at[t], ln_r.at[t], lane_at(t))
        copy.start()
        ln_copies.append(copy)
    x_copies = [None]
    for t in range(1, half):
        copy = remote(gat.at[0], gat.at[t], x_s.at[t], x_r.at[t], lane_at(2 * t))
        copy.start()
        x_copies.append(copy)
    for copy in ln_copies:
        copy.wait()
    total_chunk = lane_buf[0]
    for t in range(1, lanes):
        total_chunk = total_chunk + lane_buf[t]
    chunk[...] = total_chunk
    tot[0] = total_chunk
    ag_copies = []
    for t in range(1, groups):
        copy = remote(chunk, tot.at[t], ag_s.at[t], ag_r.at[t], grp_at(t))
        copy.start()
        ag_copies.append(copy)
    sib_copies[0].wait()
    widen(half)
    for copy in ag_copies:
        copy.wait()
    gram = jnp.concatenate(
        [tot[lax.rem(g - r + groups, groups)] for r in range(groups)], axis=0
    )
    whitener = eliminate(gram, node_total)
    high = whitener.astype(BF)
    rhs = jnp.concatenate([high, (whitener - high.astype(F32)).astype(BF)], axis=0)

    for t in range(1, half):
        x_copies[t].wait()
        copy = remote(gat.at[t], gat.at[half + t], f_s.at[t], f_r.at[t], (g, sibling))
        copy.start()
        sib_copies.append(copy)
    for t in range(1, half):
        widen(t)
    for t in range(1, half):
        sib_copies[t].wait()
        widen(half + t)
    source_copy.wait()

    radius = math.sqrt(width)

    def ball(c, _):
        at = pl.ds(pl.multiple_of(c * 256, 256), 256)
        picked = [
            wide[pl.ds(source_s[2 * c + r // tile, r % tile], 1), :] for r in range(256)
        ]
        pair = lax.dot_general(
            jnp.concatenate(picked, axis=0).astype(BF), rhs, (((1,), (1,)), ((), ())), preferred_element_type=F32
        )
        white = pair[:, :width] + pair[:, width:]
        squares = jnp.sum(white * white, axis=1, keepdims=True) + 1e-06
        norms = jnp.sqrt(squares)
        out[at] = (white * (jnp.tanh(norms / radius) * radius / norms)).astype(BF)
        return 0

    lax.fori_loop(0, rows // 256, ball, 0)


def body(features, tiles, tile_cols, send_index, send_count, coef, dest_lane, dest_slot):
    groups, lanes = lax.axis_size("grp"), lax.axis_size("lane")
    rows, width = features.shape
    blocks, per_block, tile, _ = tiles.shape
    bnd = send_index.shape[2]
    half = lanes // 2
    share = width // groups
    dma = pltpu.SemaphoreType.DMA
    vmem = pl.BlockSpec(memory_space=pltpu.VMEM)
    hbm = pl.BlockSpec(memory_space=pltpu.HBM)
    return pl.pallas_call(
        functools.partial(kernel, groups, lanes),
        out_shape=jax.ShapeDtypeStruct((rows, width), BF),
        in_specs=[hbm] * 8,
        out_specs=vmem,
        scratch_shapes=[
            pltpu.SMEM((per_block, blocks), jnp.int32),
            pltpu.SMEM((1, 2), jnp.int32),
            pltpu.VMEM((2, bnd), jnp.int32),
            pltpu.VMEM((ORDER + 1, width), F32),
            pltpu.VMEM((rows // 128, 128), jnp.int32),
            pltpu.VMEM((rows // 128, 128), jnp.int32),
            pltpu.VMEM((rows // 128, 128), jnp.int32),
            pltpu.SMEM((rows // 128, 128), jnp.int32),
            *[pltpu.VMEM(((rows + 2 * bnd) // tile, tile, width), BF)] * ORDER,
            pltpu.VMEM((blocks, per_block, tile, tile), BF),
            pltpu.VMEM((2 * bnd, rows), BF),
            pltpu.VMEM((ORDER, 2 * bnd // tile, tile, width), BF),
            pltpu.VMEM((rows, width), F32),
            pltpu.VMEM((rows, width), BF),
            pltpu.VMEM((lanes, rows, width), BF),
            pltpu.VMEM((lanes, rows // 128, 128), jnp.int32),
            pltpu.VMEM((groups, share, width), F32),
            pltpu.VMEM((groups, share, width), F32),
            pltpu.VMEM((lanes, share, width), F32),
            pltpu.VMEM((share, width), F32),
            pltpu.VMEM((groups, share, width), F32),
            pltpu.VMEM((lanes * rows, width), F32),
            dma((8,)),
            dma((ORDER, 2)), dma((ORDER, 2)),
            dma((lanes,)), dma((lanes,)),
            dma((groups,)), dma((groups,)),
            dma((lanes,)), dma((lanes,)),
            dma((groups,)), dma((groups,)),
            dma((half,)), dma((half,)),
            dma((half,)), dma((half,)),
        ],
        compiler_params=pltpu.CompilerParams(
            collective_id=0, has_side_effects=True, vmem_limit_bytes=61 * 1024 * 1024
        ),
    )(
        tile_cols.T, send_count, features.reshape(-1, tile, width), tiles, send_index.reshape(2, bnd), coef,
        dest_lane.reshape(-1, 128), dest_slot.reshape(-1, 128),
    )


def solution(mesh):
    placed = (
        P(("grp", "lane"), None),
        P(("grp", "lane"), None, None, None),
        P(("grp", "lane"), None),
        P(("grp", "lane"), None, None),
        P(("grp", "lane"), None),
        P(),
        P(("grp", "lane")),
        P(("grp", "lane")),
    )
    return jax.shard_map(
        body, mesh=mesh, in_specs=placed, out_specs=P(("grp", "lane"), None), check_vma=False
    )
```

```python
import functools
import math

import jax
import jax.numpy as jnp
from jax import lax
from jax.experimental import pallas as pl
from jax.experimental.pallas import tpu as pltpu
from jax.sharding import PartitionSpec as P

MESH = pl.DeviceIdType.MESH
BF = jnp.bfloat16
F32 = jnp.float32
ORDER = 3
SUB = 8
PIVOTS = 16


def onehot(flags):
    return jnp.where(flags, 1.0, 0.0).astype(BF)


def splat(rows, at, axis):
    return jnp.broadcast_to(lax.slice_in_dim(rows, at, at + 1, axis=axis), (SUB, rows.shape[1]))


def eliminate(state, first_lane, root):
    height, size = state.shape
    parts = PIVOTS // SUB
    lane = lax.broadcasted_iota(jnp.int32, (SUB, size), 1)
    sub = lax.broadcasted_iota(jnp.int32, (SUB, size), 0)
    result = []
    for first in range(0, height, PIVOTS):
        last = first + PIVOTS
        base = first_lane + first
        block = [state[SUB * v : SUB * (v + 1), :] for v in range(parts)]
        cols = [[splat(block[v], base + q, 1) for v in range(parts)] for q in range(PIVOTS)]
        rows = [jnp.zeros((SUB, size), F32) for _ in range(parts)]
        for r in range(PIVOTS):
            own, row = divmod(r, SUB)
            here = lane == base + r
            col = cols[r]
            pivot = splat(col[own], row, 0)
            inverse = 1.0 / pivot
            pivot_row = splat(block[own], row, 0)
            forward = jnp.where(here, 1.0, jnp.where(lane < base + r, pivot_row, 0.0))
            rows[own] = jnp.where(sub == row, forward * (root * lax.rsqrt(pivot)), rows[own])
            scaled = jnp.where(here, 1.0, pivot_row) * inverse
            for v in range(parts):
                kept = jnp.where(here, 0.0, block[v]) - col[v] * scaled
                block[v] = jnp.where(sub == row, scaled, kept) if v == own else kept
            for q in range(r + 1, PIVOTS):
                factor = splat(cols[q][own], row, 0) * inverse
                for v in range(parts):
                    kept = cols[q][v] - col[v] * factor
                    cols[q][v] = jnp.where(sub == row, factor, kept) if v == own else kept
        result += rows
        if last < height:
            rest = state[PIVOTS:, :]
            pad = block
            if base:
                pad = [jnp.zeros((base, size), F32)] + pad
            pad = pad + [jnp.zeros((size - base - PIVOTS, size), F32)]
            update = exact_dot(rest, jnp.concatenate(pad, axis=0), 1, 0)
            at = lax.broadcasted_iota(jnp.int32, rest.shape, 1)
            state = jnp.where((at >= base) & (at < base + PIVOTS), 0.0, rest) - update
    return jnp.concatenate(result, axis=0)


def exact_dot(a, b, over_a, over_b):
    return lax.dot_general(
        a, b, (((over_a,), (over_b,)), ((), ())), precision=lax.Precision.HIGHEST, preferred_element_type=F32
    )


def kernel(
    groups, lanes, wide_x, cols_h, counts_h, feats, tiles, index_h, coef_h, dest_lane_h, dest_slot_h, out,
    cols, counts, index, coef, dest_lane, dest_slot, source_v, source_s,
    ext_a0, ext_a1, ext_a2, ext_b0, ext_b1, ext_b2, tile_v, pick, quarter, fields, snd, mixed, high, low,
    gat, codes, part_a, part_b, near_a, near_b, sum_a, sum_b, far_a, far_b, tot_a, tot_b, wide,
    load_sem, halo_s, halo_r, code_s, code_r, n_s, n_r, z_s, z_r, t_s, t_r, x_s, x_r, f_s, f_r,
):
    g, l = lax.axis_index("grp"), lax.axis_index("lane")
    own_blocks, tile, width = feats.shape
    rows = own_blocks * tile
    ext = ((ext_a0, ext_a1, ext_a2), (ext_b0, ext_b1, ext_b2))
    per_block = tiles.shape[1]
    bnd = index_h.shape[1]
    lists = bnd // tile
    part_rows = rows // 4
    cut = width // 2
    root = math.sqrt(rows * groups * lanes)
    half = lanes // 2
    core = lax.rem(l, 2)
    sibling = l + 1 - 2 * core
    deep_z = groups // wide_x
    x = lax.rem(g, wide_x)
    z = lax.div(g, wide_x)

    def grp_at(t):
        return (lax.rem(g + t + groups, groups), l)

    def lane_at(t):
        return (g, lax.rem(l + t + lanes, lanes))

    def near_at(t):
        dx, dl = divmod(t, lanes)
        return (z * wide_x + lax.rem(x + dx, wide_x), lax.rem(l + dl, lanes))

    def far_at(t):
        return (lax.rem(z + t, deep_z) * wide_x + x, l)

    load_tiles = pltpu.make_async_copy(tiles, tile_v, load_sem.at[0])
    load_feats = [
        pltpu.make_async_copy(feats, ext[h][0].at[pl.ds(0, own_blocks)], load_sem.at[1 + h]) for h in range(2)
    ]
    small = [
        pltpu.make_async_copy(src, dst, load_sem.at[3 + i])
        for i, (src, dst) in enumerate(
            [
                (index_h, index), (counts_h, counts), (dest_lane_h, dest_lane),
                (dest_slot_h, dest_slot), (cols_h, cols), (coef_h, coef),
            ]
        )
    ]
    for copy in small[:2] + load_feats + small[2:] + [load_tiles]:
        copy.start()

    barrier = pltpu.get_barrier_semaphore()
    greeted = [near_at(t) for t in range(1, wide_x * lanes)] + [far_at(t) for t in range(1, deep_z)]
    greeted += [grp_at(1), grp_at(-1)]
    for peer in greeted:
        pl.semaphore_signal(barrier, inc=1, device_id=peer, device_id_type=MESH)

    row_pos = lax.broadcasted_iota(jnp.int32, (tile, tile), 0)
    lane_pos = lax.broadcasted_iota(jnp.int32, (tile, tile), 1)
    lower = lane_pos < cut

    def turn(value):
        return pltpu.roll(value, cut, 1)

    def merge(h, first, second):
        if h == 0:
            return jnp.where(lower, first, turn(second))
        return jnp.where(lower, turn(first), second)

    small[0].wait()
    small[1].wait()
    for d in range(2):
        for c in range(lists):
            at = d * bnd + c * tile
            wanted = jnp.broadcast_to(index[d : d + 1, c * tile : (c + 1) * tile], (tile, tile)).T
            quarter[pl.ds(at, tile), :] = wanted // part_rows
            inside = jnp.where(
                row_pos + c * tile < counts[0, d], jnp.bitwise_and(wanted, part_rows - 1), -1
            )
            for r in range(part_rows // tile):
                pick[pl.ds(at, tile), pl.ds(r * tile, tile)] = onehot(inside == lane_pos + r * tile)

    quads = own_blocks // 4

    def keep_fields(h, b, first, second):
        side, at = divmod(b, 2 * quads)
        fields[h, pl.ds(at * tile, tile), pl.ds(side * width, width)] = merge(h, first, second).astype(BF)

    for copy in load_feats:
        copy.wait()
    for b in (*range(quads), *range(2 * quads, 3 * quads)):
        first, second = ext_a0[b].astype(F32), ext_a0[b + quads].astype(F32)
        keep_fields(0, b, first, second)
        keep_fields(1, b, first, second)
    pl.semaphore_wait(barrier, len(greeted))

    def remote(src, dst, s, r, device):
        return pltpu.make_async_remote_copy(
            src_ref=src, dst_ref=dst, send_sem=s, recv_sem=r, device_id=device, device_id_type=MESH
        )

    middle = bnd // 2
    pair_lower = lax.broadcasted_iota(jnp.int32, (middle, width), 1) < cut

    def halo(k, h):
        copies = []
        for d in range(2):
            at = pl.ds(d * bnd, bnd)
            found = jnp.dot(pick[at, :], fields[h], preferred_element_type=F32)
            where_from = quarter[at, :]
            value = jnp.where(where_from >= 2, found[:, width:], found[:, :width])
            turned = turn(value)
            odd = jnp.bitwise_and(where_from, 1) == 1
            packed = jnp.where(
                pair_lower,
                jnp.where(odd, turned, value)[:middle],
                jnp.where(odd, value, turned)[middle:],
            ).astype(BF)
            for i in range(lists // 2):
                snd[k, h, d * (lists // 2) + i] = packed[i * tile : (i + 1) * tile]
            copy = remote(
                snd.at[k, h, pl.ds(d * (lists // 2), lists // 2)],
                ext[h][k].at[pl.ds(own_blocks + d * lists + h * (lists // 2), lists // 2)],
                halo_s.at[k, h, d], halo_r.at[k, h, d], grp_at(1 - 2 * d),
            )
            copy.start()
            copies.append(copy)
        return copies

    def unpack(k, h):
        for d in range(2):
            for i in range(lists // 2):
                at = own_blocks + d * lists + i
                here, there = (at, at + lists // 2) if h == 0 else (at + lists // 2, at)
                ext[h][k][there] = turn(ext[h][k][here].astype(F32)).astype(BF)

    def passed_code(t):
        return lax.rem(l - sibling + 2 * t + lanes, lanes)

    def invert():
        found = jnp.zeros((2 * own_blocks, tile), F32)
        high_pos = lax.broadcasted_iota(jnp.int32, (own_blocks, tile), 0)
        low_pos = lax.broadcasted_iota(jnp.int32, (own_blocks, tile), 1).astype(F32)
        for s in range(lanes):
            code = codes[passed_code(s - half) if s >= half else 2 * s] - l * rows
            left, right = [], []
            for r in range(own_blocks):
                one = code[r : r + 1, :]
                hit = jnp.where(one // tile == high_pos, 1.0, 0.0)
                left.append(
                    jnp.concatenate([hit * float(s * own_blocks + r), hit * low_pos], axis=0).astype(BF)
                )
                right.append(onehot(row_pos == jnp.bitwise_and(one, tile - 1)))
            found = found + lax.dot_general(
                jnp.concatenate(left, axis=1), jnp.concatenate(right, axis=1),
                (((1,), (1,)), ((), ())), preferred_element_type=F32,
            )
        source = found[:own_blocks] * float(tile) + found[own_blocks:]
        source_v[...] = jnp.clip(source.astype(jnp.int32), 0, lanes * rows - 1)
        copy = pltpu.make_async_copy(source_v, source_s, load_sem.at[9])
        copy.start()
        return copy

    def block(k, h, b):
        lhs = jnp.concatenate([tile_v[b, j] for j in range(per_block)], axis=1)
        rhs = jnp.concatenate([ext[h][k - 1][cols[j, b]] for j in range(per_block)], axis=0)
        value = jnp.dot(lhs, rhs, preferred_element_type=F32)
        if k > 1:
            value = 2.0 * value - ext[h][k - 2][b].astype(F32)
        term = value.astype(BF)
        wide_term = term.astype(F32)
        at = pl.ds(b * tile, tile)
        total = coef[0:1, :] * ext[h][0][b].astype(F32) if k == 1 else mixed[h, at]
        total = total + coef[k : k + 1, :] * wide_term
        if k < ORDER:
            ext[h][k][b] = term
            mixed[h, at] = total
            return wide_term
        top = total.astype(BF)
        wide_top = top.astype(F32)
        rest = total - wide_top
        if h:
            wide_high = jnp.where(lower, high[at].astype(F32), wide_top)
            rest = jnp.where(lower, low[at].astype(F32), rest)
            high[at] = wide_high.astype(BF)
        else:
            high[at] = top
        low[at] = rest.astype(BF)
        return wide_top

    def square():
        step = 512
        found = jnp.zeros((2 * width, 2 * width), F32)
        for c in range(rows // step):
            both = jnp.concatenate([high[pl.ds(c * step, step)], low[pl.ds(c * step, step)]], axis=1)
            found = found + lax.dot_general(
                both, both, (((0,), (0,)), ((), ())), preferred_element_type=F32
            )
        return (found[:width, :width] + found[width:, width:]) + (
            found[:width, width:] + found[width:, :width]
        )

    def near_start(n, part, near):
        copies = []
        for t in range(1, wide_x * lanes):
            peer = near_at(t)
            copy = remote(part.at[lax.rem(peer[1], 2)], near.at[t], n_s.at[n, t], n_r.at[n, t], peer)
            copy.start()
            copies.append(copy)
        return copies

    def far_start(n, part, near, summed, far, copies):
        for copy in copies:
            copy.wait()
        total = part[core]
        for t in range(1, wide_x * lanes):
            total = total + near[t]
        summed[...] = total
        copies = []
        for t in range(1, deep_z):
            copy = remote(summed, far.at[t], z_s.at[n, t], z_r.at[n, t], far_at(t))
            copy.start()
            copies.append(copy)
        return copies

    def twin_start(n, summed, far, tot, copies):
        for copy in copies:
            copy.wait()
        total = summed[...]
        for t in range(1, deep_z):
            total = total + far[t]
        tot[core] = total
        copy = remote(tot.at[core], tot.at[core], t_s.at[n], t_r.at[n], (g, sibling))
        copy.start()
        return copy

    def relay(h):
        copies = [remote(gat.at[h, 0], gat.at[h, half], f_s.at[h, 0], f_r.at[h, 0], (g, sibling))]
        copies += [
            remote(gat.at[h, 0], gat.at[h, t], x_s.at[h, t], x_r.at[h, t], lane_at(2 * t))
            for t in range(1, half)
        ]
        for copy in copies:
            copy.start()
        return copies

    def pass_on(h, copies):
        passed = [copies[0]]
        for t in range(1, half):
            copies[t].wait()
            copy = remote(gat.at[h, t], gat.at[h, half + t], f_s.at[h, t], f_r.at[h, t], (g, sibling))
            copy.start()
            passed.append(copy)
        return passed

    half_lower = lax.broadcasted_iota(jnp.int32, (256, width), 1) < cut

    def widen(slot):
        def step(c, _):
            at = pl.multiple_of(c * 256, 256)
            first = gat[0, slot, pl.ds(at, 256)].astype(F32)
            second = gat[1, slot, pl.ds(at, 256)].astype(F32)
            wide[pl.ds(slot * rows + at, 256)] = jnp.where(half_lower, first, turn(second))
            wide[pl.ds(slot * rows + rows // 2 + at, 256)] = jnp.where(half_lower, turn(first), second)
            return 0

        lax.fori_loop(0, rows // 512, step, 0)

    halo_copies = [halo(0, 0), halo(0, 1)]
    small[2].wait()
    small[3].wait()
    codes[0] = dest_lane[...] * rows + dest_slot[...]
    code_copies = []
    for t in range(1, lanes):
        copy = remote(codes.at[0], codes.at[t], code_s.at[t], code_r.at[t], lane_at(t))
        copy.start()
        code_copies.append(copy)
    load_tiles.wait()
    for copy in small[4:]:
        copy.wait()

    relayed, near_copies = [None, None], [None, None]
    for k in range(1, ORDER + 1):
        for h in range(2):
            for copy in halo_copies[h]:
                copy.wait()
            unpack(k - 1, h)
            if k < ORDER:
                for b in (*range(quads), *range(2 * quads, 3 * quads)):
                    first = block(k, h, b)
                    keep_fields(h, b, first, block(k, h, b + quads))
                halo_copies[h] = halo(k, h)
            else:
                for b in range(own_blocks // 2):
                    first = block(k, h, b)
                    gat[h, 0, pl.ds(b * tile, tile)] = merge(
                        h, first, block(k, h, b + own_blocks // 2)
                    ).astype(BF)
                if h == 0:
                    own_gram = square()
                    head, tail = own_gram[: cut // 2], own_gram[cut // 2 : cut]
                    flat = lax.broadcasted_iota(jnp.int32, (cut // 2, width), 1) < cut
                    packed = jnp.where(flat, head, turn(tail))
                    for i in range(2):
                        part_a[i] = packed[i * cut // 4 : (i + 1) * cut // 4]
                    near_copies[0] = near_start(0, part_a, near_a)
                else:
                    own_gram = square()
                    for i in range(2):
                        part_b[i] = own_gram[cut + i * cut // 2 : cut + (i + 1) * cut // 2]
                    near_copies[1] = near_start(1, part_b, near_b)
                relayed[h] = relay(h)
        if k == 1:
            for copy in code_copies:
                copy.wait()
            source_copy = invert()

    far_copies_a = far_start(0, part_a, near_a, sum_a, far_a, near_copies[0])
    far_copies_b = far_start(1, part_b, near_b, sum_b, far_b, near_copies[1])
    passed_a = pass_on(0, relayed[0])
    twin_start(0, sum_a, far_a, tot_a, far_copies_a).wait()
    packed = jnp.concatenate([tot_a[0], tot_a[1]], axis=0)
    flat = lax.broadcasted_iota(jnp.int32, (cut // 2, width), 1) < cut
    corner = jnp.concatenate([jnp.where(flat, packed, 0.0), jnp.where(flat, turn(packed), 0.0)], axis=0)
    first_rows = eliminate(corner, 0, root)
    corner_inverse = exact_dot(first_rows, first_rows, 0, 0) * (1.0 / (root * root))
    passed_b = pass_on(1, relayed[1])
    for copy in (passed_a[0], passed_b[0]):
        copy.wait()
    widen(0)
    widen(half)
    twin = twin_start(1, sum_b, far_b, tot_b, far_copies_b)
    twin.wait()
    strip = jnp.concatenate([tot_b[0], tot_b[1]], axis=0)
    scaled = exact_dot(strip, corner_inverse, 1, 0)
    strip_square = jnp.concatenate([jnp.zeros((cut, width), F32), strip], axis=0)
    taken = exact_dot(scaled, strip_square, 1, 1)
    flat = lax.broadcasted_iota(jnp.int32, (cut, width), 1) < cut
    second_rows = eliminate(jnp.where(flat, -scaled, strip - taken), cut, root)
    whitener = jnp.concatenate([first_rows, second_rows], axis=0)
    top = whitener.astype(BF)
    rhs = jnp.concatenate([top, (whitener - top.astype(F32)).astype(BF)], axis=0)

    for t in range(1, half):
        for copy in (passed_a[t], passed_b[t]):
            copy.wait()
        widen(t)
        widen(half + t)
    source_copy.wait()

    radius = math.sqrt(width)

    def ball(c, _):
        at = pl.ds(pl.multiple_of(c * 256, 256), 256)
        picked = [wide[pl.ds(source_s[2 * c + r // tile, r % tile], 1), :] for r in range(256)]
        pair = lax.dot_general(
            jnp.concatenate(picked, axis=0).astype(BF), rhs, (((1,), (1,)), ((), ())), preferred_element_type=F32
        )
        white = pair[:, :width] + pair[:, width:]
        squares = jnp.sum(white * white, axis=1, keepdims=True) + 1e-06
        shrink = lax.rsqrt(squares)
        out[at] = (white * (jnp.tanh(squares * shrink / radius) * radius * shrink)).astype(BF)
        return 0

    lax.fori_loop(0, rows // 256, ball, 0)


def body(features, tiles, tile_cols, send_index, send_count, coef, dest_lane, dest_slot):
    groups, lanes = lax.axis_size("grp"), lax.axis_size("lane")
    rows, width = features.shape
    blocks, per_block, tile, _ = tiles.shape
    bnd = send_index.shape[2]
    half = lanes // 2
    wide_x = 1 << ((groups.bit_length() - 1) // 2)
    near, far = wide_x * lanes, groups // wide_x
    cut = width // 2
    whole_ext = pltpu.VMEM(((rows + 2 * bnd) // tile, tile, width), BF)
    dma = pltpu.SemaphoreType.DMA
    vmem = pl.BlockSpec(memory_space=pltpu.VMEM)
    hbm = pl.BlockSpec(memory_space=pltpu.HBM)
    return pl.pallas_call(
        functools.partial(kernel, groups, lanes, wide_x),
        out_shape=jax.ShapeDtypeStruct((rows, width), BF),
        in_specs=[hbm] * 8,
        out_specs=vmem,
        scratch_shapes=[
            pltpu.SMEM((per_block, blocks), jnp.int32),
            pltpu.SMEM((1, 2), jnp.int32),
            pltpu.VMEM((2, bnd), jnp.int32),
            pltpu.VMEM((ORDER + 1, width), F32),
            pltpu.VMEM((rows // 128, 128), jnp.int32),
            pltpu.VMEM((rows // 128, 128), jnp.int32),
            pltpu.VMEM((rows // 128, 128), jnp.int32),
            pltpu.SMEM((rows // 128, 128), jnp.int32),
            *[whole_ext] * (2 * ORDER),
            pltpu.VMEM((blocks, per_block, tile, tile), BF),
            pltpu.VMEM((2 * bnd, rows // 4), BF),
            pltpu.VMEM((2 * bnd, width), jnp.int32),
            pltpu.VMEM((2, rows // 4, 2 * width), BF),
            pltpu.VMEM((ORDER, 2, bnd // tile, tile, width), BF),
            pltpu.VMEM((2, rows, width), F32),
            pltpu.VMEM((rows, width), BF),
            pltpu.VMEM((rows, width), BF),
            pltpu.VMEM((2, lanes, rows // 2, width), BF),
            pltpu.VMEM((lanes, rows // 128, 128), jnp.int32),
            pltpu.VMEM((2, cut // 4, width), F32),
            pltpu.VMEM((2, cut // 2, width), F32),
            pltpu.VMEM((near, cut // 4, width), F32),
            pltpu.VMEM((near, cut // 2, width), F32),
            pltpu.VMEM((cut // 4, width), F32),
            pltpu.VMEM((cut // 2, width), F32),
            pltpu.VMEM((far, cut // 4, width), F32),
            pltpu.VMEM((far, cut // 2, width), F32),
            pltpu.VMEM((2, cut // 4, width), F32),
            pltpu.VMEM((2, cut // 2, width), F32),
            pltpu.VMEM((lanes * rows, width), F32),
            dma((10,)),
            dma((ORDER, 2, 2)), dma((ORDER, 2, 2)),
            dma((lanes,)), dma((lanes,)),
            dma((2, near)), dma((2, near)),
            dma((2, far)), dma((2, far)),
            dma((2,)), dma((2,)),
            dma((2, half)), dma((2, half)),
            dma((2, half)), dma((2, half)),
        ],
        compiler_params=pltpu.CompilerParams(
            collective_id=0, has_side_effects=True, vmem_limit_bytes=61 * 1024 * 1024
        ),
    )(
        tile_cols.T, send_count, features.reshape(-1, tile, width), tiles, send_index.reshape(2, bnd), coef,
        dest_lane.reshape(-1, 128), dest_slot.reshape(-1, 128),
    )


def solution(mesh):
    placed = (
        P(("grp", "lane"), None),
        P(("grp", "lane"), None, None, None),
        P(("grp", "lane"), None),
        P(("grp", "lane"), None, None),
        P(("grp", "lane"), None),
        P(),
        P(("grp", "lane")),
        P(("grp", "lane")),
    )
    return jax.shard_map(
        body, mesh=mesh, in_specs=placed, out_specs=P(("grp", "lane"), None), check_vma=False
    )
```

```python
import functools
import math

import jax
import jax.numpy as jnp
from jax import lax
from jax.experimental import pallas as pl
from jax.experimental.pallas import tpu as pltpu
from jax.sharding import PartitionSpec as P

MESH = pl.DeviceIdType.MESH
BF = jnp.bfloat16
F32 = jnp.float32
ORDER = 3
SUB = 8
PIVOTS = 16


def onehot(flags):
    return jnp.where(flags, 1.0, 0.0).astype(BF)


def splat(rows, at, axis):
    return jnp.broadcast_to(lax.slice_in_dim(rows, at, at + 1, axis=axis), (SUB, rows.shape[1]))


def eliminate(state, first_lane, root):
    height, size = state.shape
    parts = PIVOTS // SUB
    lane = lax.broadcasted_iota(jnp.int32, (SUB, size), 1)
    sub = lax.broadcasted_iota(jnp.int32, (SUB, size), 0)
    result = []
    for first in range(0, height, PIVOTS):
        last = first + PIVOTS
        base = first_lane + first
        block = [state[SUB * v : SUB * (v + 1), :] for v in range(parts)]
        cols = [[splat(block[v], base + q, 1) for v in range(parts)] for q in range(PIVOTS)]
        rows = [jnp.zeros((SUB, size), F32) for _ in range(parts)]
        for r in range(PIVOTS):
            own, row = divmod(r, SUB)
            here = lane == base + r
            col = cols[r]
            pivot = splat(col[own], row, 0)
            inverse = 1.0 / pivot
            pivot_row = splat(block[own], row, 0)
            forward = jnp.where(here, 1.0, jnp.where(lane < base + r, pivot_row, 0.0))
            rows[own] = jnp.where(sub == row, forward * (root * lax.rsqrt(pivot)), rows[own])
            scaled = jnp.where(here, 1.0, pivot_row) * inverse
            for v in range(parts):
                kept = jnp.where(here, 0.0, block[v]) - col[v] * scaled
                block[v] = jnp.where(sub == row, scaled, kept) if v == own else kept
            for q in range(r + 1, PIVOTS):
                factor = splat(cols[q][own], row, 0) * inverse
                for v in range(parts):
                    kept = cols[q][v] - col[v] * factor
                    cols[q][v] = jnp.where(sub == row, factor, kept) if v == own else kept
        result += rows
        if last < height:
            rest = state[PIVOTS:, :]
            pad = block
            if base:
                pad = [jnp.zeros((base, size), F32)] + pad
            pad = pad + [jnp.zeros((size - base - PIVOTS, size), F32)]
            update = exact_dot(rest, jnp.concatenate(pad, axis=0), 1, 0)
            at = lax.broadcasted_iota(jnp.int32, rest.shape, 1)
            state = jnp.where((at >= base) & (at < base + PIVOTS), 0.0, rest) - update
    return jnp.concatenate(result, axis=0)


def exact_dot(a, b, over_a, over_b):
    return lax.dot_general(
        a, b, (((over_a,), (over_b,)), ((), ())), precision=lax.Precision.HIGHEST, preferred_element_type=F32
    )


def kernel(
    groups, lanes, wide_x, cols_h, counts_h, feats, tiles, index_h, coef_h, dest_lane_h, dest_slot_h, out,
    cols, counts, index, coef, dest_lane, dest_slot, source_v, source_s,
    ext_a0, ext_a1, ext_a2, ext_b0, ext_b1, ext_b2, tile_v, pick, quarter, fields, snd, mixed, high, low,
    gat, codes, part_a, part_b, near_a, near_b, sum_a, sum_b, far_a, far_b, tot_a, tot_b, wide,
    load_sem, halo_s, halo_r, code_s, code_r, n_s, n_r, z_s, z_r, t_s, t_r, x_s, x_r, f_s, f_r,
):
    g, l = lax.axis_index("grp"), lax.axis_index("lane")
    own_blocks, tile, width = feats.shape
    rows = own_blocks * tile
    ext = ((ext_a0, ext_a1, ext_a2), (ext_b0, ext_b1, ext_b2))
    per_block = tiles.shape[1]
    bnd = index_h.shape[1]
    lists = bnd // tile
    part_rows = rows // 4
    cut = width // 2
    root = math.sqrt(rows * groups * lanes)
    half = lanes // 2
    core = lax.rem(l, 2)
    sibling = l + 1 - 2 * core
    deep_z = groups // wide_x
    x = lax.rem(g, wide_x)
    z = lax.div(g, wide_x)

    def grp_at(t):
        return (lax.rem(g + t + groups, groups), l)

    def lane_at(t):
        return (g, lax.rem(l + t + lanes, lanes))

    def near_at(t):
        dx, dl = divmod(t, lanes)
        return (z * wide_x + lax.rem(x + dx, wide_x), lax.rem(l + dl, lanes))

    def far_at(t):
        return (lax.rem(z + t, deep_z) * wide_x + x, l)

    load_tiles = pltpu.make_async_copy(tiles, tile_v, load_sem.at[0])
    load_feats = [
        pltpu.make_async_copy(feats, ext[h][0].at[pl.ds(0, own_blocks)], load_sem.at[1 + h]) for h in range(2)
    ]
    small = [
        pltpu.make_async_copy(src, dst, load_sem.at[3 + i])
        for i, (src, dst) in enumerate(
            [
                (index_h, index), (counts_h, counts), (dest_lane_h, dest_lane),
                (dest_slot_h, dest_slot), (cols_h, cols), (coef_h, coef),
            ]
        )
    ]
    for copy in small[:2] + load_feats + small[2:] + [load_tiles]:
        copy.start()

    barrier = pltpu.get_barrier_semaphore()
    greeted = [near_at(t) for t in range(1, wide_x * lanes)] + [far_at(t) for t in range(1, deep_z)]
    greeted += [grp_at(1), grp_at(-1)]
    for peer in greeted:
        pl.semaphore_signal(barrier, inc=1, device_id=peer, device_id_type=MESH)

    row_pos = lax.broadcasted_iota(jnp.int32, (tile, tile), 0)
    lane_pos = lax.broadcasted_iota(jnp.int32, (tile, tile), 1)
    lower = lane_pos < cut

    def turn(value):
        return pltpu.roll(value, cut, 1)

    def merge(h, first, second):
        if h == 0:
            return jnp.where(lower, first, turn(second))
        return jnp.where(lower, turn(first), second)

    small[0].wait()
    small[1].wait()
    for d in range(2):
        for c in range(lists):
            at = d * bnd + c * tile
            wanted = jnp.broadcast_to(index[d : d + 1, c * tile : (c + 1) * tile], (tile, tile)).T
            quarter[pl.ds(at, tile), :] = wanted // part_rows
            inside = jnp.where(
                row_pos + c * tile < counts[0, d], jnp.bitwise_and(wanted, part_rows - 1), -1
            )
            for r in range(part_rows // tile):
                pick[pl.ds(at, tile), pl.ds(r * tile, tile)] = onehot(inside == lane_pos + r * tile)

    quads = own_blocks // 4

    def keep_fields(h, b, first, second):
        side, at = divmod(b, 2 * quads)
        fields[h, pl.ds(at * tile, tile), pl.ds(side * width, width)] = merge(h, first, second).astype(BF)

    for copy in load_feats:
        copy.wait()
    for b in (*range(quads), *range(2 * quads, 3 * quads)):
        first, second = ext_a0[b].astype(F32), ext_a0[b + quads].astype(F32)
        keep_fields(0, b, first, second)
        keep_fields(1, b, first, second)
    pl.semaphore_wait(barrier, len(greeted))

    def remote(src, dst, s, r, device):
        return pltpu.make_async_remote_copy(
            src_ref=src, dst_ref=dst, send_sem=s, recv_sem=r, device_id=device, device_id_type=MESH
        )

    middle = bnd // 2
    pair_lower = lax.broadcasted_iota(jnp.int32, (middle, width), 1) < cut

    def halo(k, h):
        copies = []
        for d in range(2):
            at = pl.ds(d * bnd, bnd)
            found = jnp.dot(pick[at, :], fields[h], preferred_element_type=F32)
            where_from = quarter[at, :]
            value = jnp.where(where_from >= 2, found[:, width:], found[:, :width])
            turned = turn(value)
            odd = jnp.bitwise_and(where_from, 1) == 1
            packed = jnp.where(
                pair_lower,
                jnp.where(odd, turned, value)[:middle],
                jnp.where(odd, value, turned)[middle:],
            ).astype(BF)
            for i in range(lists // 2):
                snd[k, h, d * (lists // 2) + i] = packed[i * tile : (i + 1) * tile]
            copy = remote(
                snd.at[k, h, pl.ds(d * (lists // 2), lists // 2)],
                ext[h][k].at[pl.ds(own_blocks + d * lists + h * (lists // 2), lists // 2)],
                halo_s.at[k, h, d], halo_r.at[k, h, d], grp_at(1 - 2 * d),
            )
            copy.start()
            copies.append(copy)
        return copies

    def unpack(k, h):
        for d in range(2):
            for i in range(lists // 2):
                at = own_blocks + d * lists + i
                here, there = (at, at + lists // 2) if h == 0 else (at + lists // 2, at)
                ext[h][k][there] = turn(ext[h][k][here].astype(F32)).astype(BF)

    def passed_code(t):
        return lax.rem(l - sibling + 2 * t + lanes, lanes)

    def invert():
        found = jnp.zeros((2 * own_blocks, tile), F32)
        high_pos = lax.broadcasted_iota(jnp.int32, (own_blocks, tile), 0)
        low_pos = lax.broadcasted_iota(jnp.int32, (own_blocks, tile), 1).astype(F32)
        for s in range(lanes):
            code = codes[passed_code(s - half) if s >= half else 2 * s] - l * rows
            left, right = [], []
            for r in range(own_blocks):
                one = code[r : r + 1, :]
                hit = jnp.where(one // tile == high_pos, 1.0, 0.0)
                left.append(
                    jnp.concatenate([hit * float(s * own_blocks + r), hit * low_pos], axis=0).astype(BF)
                )
                right.append(onehot(row_pos == jnp.bitwise_and(one, tile - 1)))
            found = found + lax.dot_general(
                jnp.concatenate(left, axis=1), jnp.concatenate(right, axis=1),
                (((1,), (1,)), ((), ())), preferred_element_type=F32,
            )
        source = found[:own_blocks] * float(tile) + found[own_blocks:]
        source_v[...] = jnp.clip(source.astype(jnp.int32), 0, lanes * rows - 1)
        copy = pltpu.make_async_copy(source_v, source_s, load_sem.at[9])
        copy.start()
        return copy

    def block(k, h, b):
        lhs = jnp.concatenate([tile_v[b, j] for j in range(per_block)], axis=1)
        rhs = jnp.concatenate([ext[h][k - 1][cols[j, b]] for j in range(per_block)], axis=0)
        value = jnp.dot(lhs, rhs, preferred_element_type=F32)
        if k > 1:
            value = 2.0 * value - ext[h][k - 2][b].astype(F32)
        term = value.astype(BF)
        wide_term = term.astype(F32)
        at = pl.ds(b * tile, tile)
        total = coef[0:1, :] * ext[h][0][b].astype(F32) if k == 1 else mixed[h, at]
        total = total + coef[k : k + 1, :] * wide_term
        if k < ORDER:
            ext[h][k][b] = term
            mixed[h, at] = total
            return wide_term
        top = total.astype(BF)
        wide_top = top.astype(F32)
        rest = total - wide_top
        if h:
            wide_high = jnp.where(lower, high[at].astype(F32), wide_top)
            rest = jnp.where(lower, low[at].astype(F32), rest)
            high[at] = wide_high.astype(BF)
        else:
            high[at] = top
        low[at] = rest.astype(BF)
        return wide_top

    def square():
        step = 512
        found = jnp.zeros((2 * width, 2 * width), F32)
        for c in range(rows // step):
            both = jnp.concatenate([high[pl.ds(c * step, step)], low[pl.ds(c * step, step)]], axis=1)
            found = found + lax.dot_general(
                both, both, (((0,), (0,)), ((), ())), preferred_element_type=F32
            )
        return (found[:width, :width] + found[width:, width:]) + (
            found[:width, width:] + found[width:, :width]
        )

    def near_start(n, part, near):
        copies = []
        for t in range(1, wide_x * lanes):
            peer = near_at(t)
            copy = remote(part.at[lax.rem(peer[1], 2)], near.at[t], n_s.at[n, t], n_r.at[n, t], peer)
            copy.start()
            copies.append(copy)
        return copies

    def far_start(n, part, near, summed, far, copies):
        for copy in copies:
            copy.wait()
        total = part[core]
        for t in range(1, wide_x * lanes):
            total = total + near[t]
        summed[...] = total
        copies = []
        for t in range(1, deep_z):
            copy = remote(summed, far.at[t], z_s.at[n, t], z_r.at[n, t], far_at(t))
            copy.start()
            copies.append(copy)
        return copies

    def twin_start(n, summed, far, tot, copies):
        for copy in copies:
            copy.wait()
        total = summed[...]
        for t in range(1, deep_z):
            total = total + far[t]
        tot[core] = total
        copy = remote(tot.at[core], tot.at[core], t_s.at[n], t_r.at[n], (g, sibling))
        copy.start()
        return copy

    def relay(h):
        copies = [remote(gat.at[h, 0], gat.at[h, half], f_s.at[h, 0], f_r.at[h, 0], (g, sibling))]
        copies += [
            remote(gat.at[h, 0], gat.at[h, t], x_s.at[h, t], x_r.at[h, t], lane_at(2 * t))
            for t in range(1, half)
        ]
        for copy in copies:
            copy.start()
        return copies

    def pass_on(h, copies):
        passed = [copies[0]]
        for t in range(1, half):
            copies[t].wait()
            copy = remote(gat.at[h, t], gat.at[h, half + t], f_s.at[h, t], f_r.at[h, t], (g, sibling))
            copy.start()
            passed.append(copy)
        return passed

    half_lower = lax.broadcasted_iota(jnp.int32, (256, width), 1) < cut

    def widen(slot):
        def step(c, _):
            at = pl.multiple_of(c * 256, 256)
            first = gat[0, slot, pl.ds(at, 256)].astype(F32)
            second = gat[1, slot, pl.ds(at, 256)].astype(F32)
            wide[pl.ds(slot * rows + at, 256)] = jnp.where(half_lower, first, turn(second))
            wide[pl.ds(slot * rows + rows // 2 + at, 256)] = jnp.where(half_lower, turn(first), second)
            return 0

        lax.fori_loop(0, rows // 512, step, 0)

    halo_copies = [halo(0, 0), halo(0, 1)]
    small[2].wait()
    small[3].wait()
    codes[0] = dest_lane[...] * rows + dest_slot[...]
    code_copies = []
    for t in range(1, lanes):
        copy = remote(codes.at[0], codes.at[t], code_s.at[t], code_r.at[t], lane_at(t))
        copy.start()
        code_copies.append(copy)
    load_tiles.wait()
    for copy in small[4:]:
        copy.wait()

    relayed, near_copies = [None, None], [None, None]
    for k in range(1, ORDER + 1):
        for h in range(2):
            for copy in halo_copies[h]:
                copy.wait()
            unpack(k - 1, h)
            if k < ORDER:
                for b in (*range(quads), *range(2 * quads, 3 * quads)):
                    first = block(k, h, b)
                    keep_fields(h, b, first, block(k, h, b + quads))
                halo_copies[h] = halo(k, h)
            else:
                for b in range(own_blocks // 2):
                    first = block(k, h, b)
                    gat[h, 0, pl.ds(b * tile, tile)] = merge(
                        h, first, block(k, h, b + own_blocks // 2)
                    ).astype(BF)
                if h == 0:
                    own_gram = square()
                    head, tail = own_gram[: cut // 2], own_gram[cut // 2 : cut]
                    flat = lax.broadcasted_iota(jnp.int32, (cut // 2, width), 1) < cut
                    packed = jnp.where(flat, head, turn(tail))
                    for i in range(2):
                        part_a[i] = packed[i * cut // 4 : (i + 1) * cut // 4]
                    near_copies[0] = near_start(0, part_a, near_a)
                else:
                    own_gram = square()
                    for i in range(2):
                        part_b[i] = own_gram[cut + i * cut // 2 : cut + (i + 1) * cut // 2]
                    near_copies[1] = near_start(1, part_b, near_b)
                relayed[h] = relay(h)
        if k == 1:
            for copy in code_copies:
                copy.wait()
            source_copy = invert()

    far_copies_a = far_start(0, part_a, near_a, sum_a, far_a, near_copies[0])
    far_copies_b = far_start(1, part_b, near_b, sum_b, far_b, near_copies[1])
    passed_a = pass_on(0, relayed[0])
    twin_start(0, sum_a, far_a, tot_a, far_copies_a).wait()
    packed = jnp.concatenate([tot_a[0], tot_a[1]], axis=0)
    flat = lax.broadcasted_iota(jnp.int32, (cut // 2, width), 1) < cut
    corner = jnp.concatenate([jnp.where(flat, packed, 0.0), jnp.where(flat, turn(packed), 0.0)], axis=0)
    first_rows = eliminate(corner, 0, root)
    corner_inverse = exact_dot(first_rows, first_rows, 0, 0) * (1.0 / (root * root))
    passed_b = pass_on(1, relayed[1])
    for copy in (passed_a[0], passed_b[0]):
        copy.wait()
    widen(0)
    widen(half)
    twin = twin_start(1, sum_b, far_b, tot_b, far_copies_b)
    twin.wait()
    strip = jnp.concatenate([tot_b[0], tot_b[1]], axis=0)
    scaled = exact_dot(strip, corner_inverse, 1, 0)
    strip_square = jnp.concatenate([jnp.zeros((cut, width), F32), strip], axis=0)
    taken = exact_dot(scaled, strip_square, 1, 1)
    flat = lax.broadcasted_iota(jnp.int32, (cut, width), 1) < cut
    second_rows = eliminate(jnp.where(flat, -scaled, strip - taken), cut, root)
    whitener = jnp.concatenate([first_rows, second_rows], axis=0)
    top = whitener.astype(BF)
    rhs = jnp.concatenate([top, (whitener - top.astype(F32)).astype(BF)], axis=0)

    for t in range(1, half):
        for copy in (passed_a[t], passed_b[t]):
            copy.wait()
        widen(t)
        widen(half + t)
    source_copy.wait()

    radius = math.sqrt(width)
    ones = jnp.ones((2 * width, width), BF)

    def ball(c, _):
        at = pl.ds(pl.multiple_of(c * 256, 256), 256)
        picked = [wide[pl.ds(source_s[2 * c + r // tile, r % tile], 1), :] for r in range(256)]
        pair = lax.dot_general(
            jnp.concatenate(picked, axis=0).astype(BF), rhs, (((1,), (1,)), ((), ())), preferred_element_type=F32
        )
        white = pair[:, :width] + pair[:, width:]
        each = white * white
        head = each.astype(BF)
        parts = jnp.concatenate([head, (each - head.astype(F32)).astype(BF)], axis=1)
        squares = jnp.dot(parts, ones, preferred_element_type=F32) + 1e-06
        shrink = lax.rsqrt(squares)
        out[at] = (white * (jnp.tanh(squares * shrink / radius) * radius * shrink)).astype(BF)
        return 0

    lax.fori_loop(0, rows // 256, ball, 0, unroll=2)


def body(features, tiles, tile_cols, send_index, send_count, coef, dest_lane, dest_slot):
    groups, lanes = lax.axis_size("grp"), lax.axis_size("lane")
    rows, width = features.shape
    blocks, per_block, tile, _ = tiles.shape
    bnd = send_index.shape[2]
    half = lanes // 2
    wide_x = 1 << ((groups.bit_length() - 1) // 2)
    near, far = wide_x * lanes, groups // wide_x
    cut = width // 2
    whole_ext = pltpu.VMEM(((rows + 2 * bnd) // tile, tile, width), BF)
    dma = pltpu.SemaphoreType.DMA
    vmem = pl.BlockSpec(memory_space=pltpu.VMEM)
    hbm = pl.BlockSpec(memory_space=pltpu.HBM)
    return pl.pallas_call(
        functools.partial(kernel, groups, lanes, wide_x),
        out_shape=pltpu.VMEM((rows, width), BF),
        in_specs=[hbm] * 8,
        out_specs=vmem,
        scratch_shapes=[
            pltpu.SMEM((per_block, blocks), jnp.int32),
            pltpu.SMEM((1, 2), jnp.int32),
            pltpu.VMEM((2, bnd), jnp.int32),
            pltpu.VMEM((ORDER + 1, width), F32),
            pltpu.VMEM((rows // 128, 128), jnp.int32),
            pltpu.VMEM((rows // 128, 128), jnp.int32),
            pltpu.VMEM((rows // 128, 128), jnp.int32),
            pltpu.SMEM((rows // 128, 128), jnp.int32),
            *[whole_ext] * (2 * ORDER),
            pltpu.VMEM((blocks, per_block, tile, tile), BF),
            pltpu.VMEM((2 * bnd, rows // 4), BF),
            pltpu.VMEM((2 * bnd, width), jnp.int32),
            pltpu.VMEM((2, rows // 4, 2 * width), BF),
            pltpu.VMEM((ORDER, 2, bnd // tile, tile, width), BF),
            pltpu.VMEM((2, rows, width), F32),
            pltpu.VMEM((rows, width), BF),
            pltpu.VMEM((rows, width), BF),
            pltpu.VMEM((2, lanes, rows // 2, width), BF),
            pltpu.VMEM((lanes, rows // 128, 128), jnp.int32),
            pltpu.VMEM((2, cut // 4, width), F32),
            pltpu.VMEM((2, cut // 2, width), F32),
            pltpu.VMEM((near, cut // 4, width), F32),
            pltpu.VMEM((near, cut // 2, width), F32),
            pltpu.VMEM((cut // 4, width), F32),
            pltpu.VMEM((cut // 2, width), F32),
            pltpu.VMEM((far, cut // 4, width), F32),
            pltpu.VMEM((far, cut // 2, width), F32),
            pltpu.VMEM((2, cut // 4, width), F32),
            pltpu.VMEM((2, cut // 2, width), F32),
            pltpu.VMEM((lanes * rows, width), F32),
            dma((10,)),
            dma((ORDER, 2, 2)), dma((ORDER, 2, 2)),
            dma((lanes,)), dma((lanes,)),
            dma((2, near)), dma((2, near)),
            dma((2, far)), dma((2, far)),
            dma((2,)), dma((2,)),
            dma((2, half)), dma((2, half)),
            dma((2, half)), dma((2, half)),
        ],
        compiler_params=pltpu.CompilerParams(
            collective_id=0, has_side_effects=True, vmem_limit_bytes=61 * 1024 * 1024
        ),
    )(
        tile_cols.T, send_count, features.reshape(-1, tile, width), tiles, send_index.reshape(2, bnd), coef,
        dest_lane.reshape(-1, 128), dest_slot.reshape(-1, 128),
    )


def solution(mesh):
    placed = (
        P(("grp", "lane"), None),
        P(("grp", "lane"), None, None, None),
        P(("grp", "lane"), None),
        P(("grp", "lane"), None, None),
        P(("grp", "lane"), None),
        P(),
        P(("grp", "lane")),
        P(("grp", "lane")),
    )
    return jax.shard_map(
        body, mesh=mesh, in_specs=placed, out_specs=P(("grp", "lane"), None), check_vma=False
    )
```

```python
import functools
import math

import jax
import jax.numpy as jnp
from jax import lax
from jax.experimental import pallas as pl
from jax.experimental.pallas import tpu as pltpu
from jax.sharding import PartitionSpec as P

MESH = pl.DeviceIdType.MESH
BF = jnp.bfloat16
F32 = jnp.float32
ORDER = 3
SUB = 8
PIVOTS = 16


def onehot(flags):
    return jnp.where(flags, 1.0, 0.0).astype(BF)


def splat(rows, at, axis):
    return jnp.broadcast_to(lax.slice_in_dim(rows, at, at + 1, axis=axis), (SUB, rows.shape[1]))


def eliminate(state, first_lane, root):
    height, size = state.shape
    parts = PIVOTS // SUB
    lane = lax.broadcasted_iota(jnp.int32, (SUB, size), 1)
    sub = lax.broadcasted_iota(jnp.int32, (SUB, size), 0)
    result = []
    for first in range(0, height, PIVOTS):
        last = first + PIVOTS
        base = first_lane + first
        block = [state[SUB * v : SUB * (v + 1), :] for v in range(parts)]
        cols = [[splat(block[v], base + q, 1) for v in range(parts)] for q in range(PIVOTS)]
        rows = [jnp.zeros((SUB, size), F32) for _ in range(parts)]
        for r in range(PIVOTS):
            own, row = divmod(r, SUB)
            here = lane == base + r
            col = cols[r]
            pivot = splat(col[own], row, 0)
            inverse = 1.0 / pivot
            pivot_row = splat(block[own], row, 0)
            forward = jnp.where(here, 1.0, jnp.where(lane < base + r, pivot_row, 0.0))
            rows[own] = jnp.where(sub == row, forward * (root * lax.rsqrt(pivot)), rows[own])
            scaled = jnp.where(here, 1.0, pivot_row) * inverse
            for v in range(parts):
                kept = jnp.where(here, 0.0, block[v]) - col[v] * scaled
                block[v] = jnp.where(sub == row, scaled, kept) if v == own else kept
            for q in range(r + 1, PIVOTS):
                factor = splat(cols[q][own], row, 0) * inverse
                for v in range(parts):
                    kept = cols[q][v] - col[v] * factor
                    cols[q][v] = jnp.where(sub == row, factor, kept) if v == own else kept
        result += rows
        if last < height:
            rest = state[PIVOTS:, :]
            pad = block
            if base:
                pad = [jnp.zeros((base, size), F32)] + pad
            pad = pad + [jnp.zeros((size - base - PIVOTS, size), F32)]
            update = exact_dot(rest, jnp.concatenate(pad, axis=0), 1, 0)
            at = lax.broadcasted_iota(jnp.int32, rest.shape, 1)
            state = jnp.where((at >= base) & (at < base + PIVOTS), 0.0, rest) - update
    return jnp.concatenate(result, axis=0)


def exact_dot(a, b, over_a, over_b):
    return lax.dot_general(
        a, b, (((over_a,), (over_b,)), ((), ())), precision=lax.Precision.HIGHEST, preferred_element_type=F32
    )


def kernel(
    groups, lanes, wide_x, cols_h, counts_h, feats, tiles, index_h, coef_h, dest_lane_h, dest_slot_h, out,
    cols, counts, index, coef, dest_lane, dest_slot, source_v, source_s,
    ext_a0, ext_a1, ext_a2, ext_b0, ext_b1, ext_b2, tile_v, pick, quarter, fields, snd, mixed, high, low,
    gat, codes, part_a, part_b, near_a, near_b, sum_a, sum_b, far_a, far_b, tot_a, tot_b, wide,
    load_sem, halo_s, halo_r, code_s, code_r, n_s, n_r, z_s, z_r, t_s, t_r, x_s, x_r, f_s, f_r,
):
    g, l = lax.axis_index("grp"), lax.axis_index("lane")
    own_blocks, tile, width = feats.shape
    rows = own_blocks * tile
    ext = ((ext_a0, ext_a1, ext_a2), (ext_b0, ext_b1, ext_b2))
    per_block = tiles.shape[1]
    bnd = index_h.shape[1]
    lists = bnd // tile
    part_rows = rows // 4
    cut = width // 2
    root = math.sqrt(rows * groups * lanes)
    half = lanes // 2
    core = lax.rem(l, 2)
    sibling = l + 1 - 2 * core
    deep_z = groups // wide_x
    x = lax.rem(g, wide_x)
    z = lax.div(g, wide_x)

    def grp_at(t):
        return (lax.rem(g + t + groups, groups), l)

    def lane_at(t):
        return (g, lax.rem(l + t + lanes, lanes))

    def near_at(t):
        dx, dl = divmod(t, lanes)
        return (z * wide_x + lax.rem(x + dx, wide_x), lax.rem(l + dl, lanes))

    def far_at(t):
        return (lax.rem(z + t, deep_z) * wide_x + x, l)

    load_tiles = pltpu.make_async_copy(tiles, tile_v, load_sem.at[0])
    load_feats = [
        pltpu.make_async_copy(feats, ext[h][0].at[pl.ds(0, own_blocks)], load_sem.at[1 + h]) for h in range(2)
    ]
    small = [
        pltpu.make_async_copy(src, dst, load_sem.at[3 + i])
        for i, (src, dst) in enumerate(
            [
                (index_h, index), (counts_h, counts), (dest_lane_h, dest_lane),
                (dest_slot_h, dest_slot), (cols_h, cols), (coef_h, coef),
            ]
        )
    ]
    for copy in small[:2] + load_feats + small[2:] + [load_tiles]:
        copy.start()

    barrier = pltpu.get_barrier_semaphore()
    greeted = [near_at(t) for t in range(1, wide_x * lanes)] + [far_at(t) for t in range(1, deep_z)]
    greeted += [grp_at(1), grp_at(-1)]
    for peer in greeted:
        pl.semaphore_signal(barrier, inc=1, device_id=peer, device_id_type=MESH)

    row_pos = lax.broadcasted_iota(jnp.int32, (tile, tile), 0)
    lane_pos = lax.broadcasted_iota(jnp.int32, (tile, tile), 1)
    lower = lane_pos < cut

    def turn(value):
        return pltpu.roll(value, cut, 1)

    def merge(h, first, second):
        if h == 0:
            return jnp.where(lower, first, turn(second))
        return jnp.where(lower, turn(first), second)

    small[0].wait()
    small[1].wait()
    for d in range(2):
        for c in range(lists):
            at = d * bnd + c * tile
            wanted = jnp.broadcast_to(index[d : d + 1, c * tile : (c + 1) * tile], (tile, tile)).T
            quarter[pl.ds(at, tile), :] = wanted // part_rows
            inside = jnp.where(
                row_pos + c * tile < counts[0, d], jnp.bitwise_and(wanted, part_rows - 1), -1
            )
            for r in range(part_rows // tile):
                pick[pl.ds(at, tile), pl.ds(r * tile, tile)] = onehot(inside == lane_pos + r * tile)

    quads = own_blocks // 4

    def keep_fields(h, b, first, second):
        side, at = divmod(b, 2 * quads)
        fields[h, pl.ds(at * tile, tile), pl.ds(side * width, width)] = merge(h, first, second).astype(BF)

    for copy in load_feats:
        copy.wait()
    for b in (*range(quads), *range(2 * quads, 3 * quads)):
        first, second = ext_a0[b].astype(F32), ext_a0[b + quads].astype(F32)
        keep_fields(0, b, first, second)
        keep_fields(1, b, first, second)
    pl.semaphore_wait(barrier, len(greeted))

    def remote(src, dst, s, r, device):
        return pltpu.make_async_remote_copy(
            src_ref=src, dst_ref=dst, send_sem=s, recv_sem=r, device_id=device, device_id_type=MESH
        )

    middle = bnd // 2
    pair_lower = lax.broadcasted_iota(jnp.int32, (middle, width), 1) < cut

    def halo(k, h):
        copies = []
        for d in range(2):
            at = pl.ds(d * bnd, bnd)
            found = jnp.dot(pick[at, :], fields[h], preferred_element_type=F32)
            where_from = quarter[at, :]
            value = jnp.where(where_from >= 2, found[:, width:], found[:, :width])
            turned = turn(value)
            odd = jnp.bitwise_and(where_from, 1) == 1
            packed = jnp.where(
                pair_lower,
                jnp.where(odd, turned, value)[:middle],
                jnp.where(odd, value, turned)[middle:],
            ).astype(BF)
            for i in range(lists // 2):
                snd[k, h, d * (lists // 2) + i] = packed[i * tile : (i + 1) * tile]
            copy = remote(
                snd.at[k, h, pl.ds(d * (lists // 2), lists // 2)],
                ext[h][k].at[pl.ds(own_blocks + d * lists + h * (lists // 2), lists // 2)],
                halo_s.at[k, h, d], halo_r.at[k, h, d], grp_at(1 - 2 * d),
            )
            copy.start()
            copies.append(copy)
        return copies

    def unpack(k, h):
        for d in range(2):
            for i in range(lists // 2):
                at = own_blocks + d * lists + i
                here, there = (at, at + lists // 2) if h == 0 else (at + lists // 2, at)
                ext[h][k][there] = turn(ext[h][k][here].astype(F32)).astype(BF)

    def passed_code(t):
        return lax.rem(l - sibling + 2 * t + lanes, lanes)

    def invert():
        found = jnp.zeros((2 * own_blocks, tile), F32)
        high_pos = lax.broadcasted_iota(jnp.int32, (own_blocks, tile), 0)
        low_pos = lax.broadcasted_iota(jnp.int32, (own_blocks, tile), 1).astype(F32)
        for s in range(lanes):
            code = codes[passed_code(s - half) if s >= half else 2 * s] - l * rows
            left, right = [], []
            for r in range(own_blocks):
                one = code[r : r + 1, :]
                hit = jnp.where(one // tile == high_pos, 1.0, 0.0)
                left.append(
                    jnp.concatenate([hit * float(s * own_blocks + r), hit * low_pos], axis=0).astype(BF)
                )
                right.append(onehot(row_pos == jnp.bitwise_and(one, tile - 1)))
            found = found + lax.dot_general(
                jnp.concatenate(left, axis=1), jnp.concatenate(right, axis=1),
                (((1,), (1,)), ((), ())), preferred_element_type=F32,
            )
        source = found[:own_blocks] * float(tile) + found[own_blocks:]
        source_v[...] = jnp.clip(source.astype(jnp.int32), 0, lanes * rows - 1)
        copy = pltpu.make_async_copy(source_v, source_s, load_sem.at[9])
        copy.start()
        return copy

    def block(k, h, b):
        lhs = jnp.concatenate([tile_v[b, j] for j in range(per_block)], axis=1)
        rhs = jnp.concatenate([ext[h][k - 1][cols[j, b]] for j in range(per_block)], axis=0)
        value = jnp.dot(lhs, rhs, preferred_element_type=F32)
        if k > 1:
            value = 2.0 * value - ext[h][k - 2][b].astype(F32)
        term = value.astype(BF)
        wide_term = term.astype(F32)
        at = pl.ds(b * tile, tile)
        total = coef[0:1, :] * ext[h][0][b].astype(F32) if k == 1 else mixed[h, at]
        total = total + coef[k : k + 1, :] * wide_term
        if k < ORDER:
            ext[h][k][b] = term
            mixed[h, at] = total
            return wide_term
        top = total.astype(BF)
        wide_top = top.astype(F32)
        rest = total - wide_top
        if h:
            wide_high = jnp.where(lower, high[at].astype(F32), wide_top)
            rest = jnp.where(lower, low[at].astype(F32), rest)
            high[at] = wide_high.astype(BF)
        else:
            high[at] = top
        low[at] = rest.astype(BF)
        return wide_top

    def square():
        step = 512
        found = jnp.zeros((2 * width, 2 * width), F32)
        for c in range(rows // step):
            both = jnp.concatenate([high[pl.ds(c * step, step)], low[pl.ds(c * step, step)]], axis=1)
            found = found + lax.dot_general(
                both, both, (((0,), (0,)), ((), ())), preferred_element_type=F32
            )
        return (found[:width, :width] + found[width:, width:]) + (
            found[:width, width:] + found[width:, :width]
        )

    def near_start(n, part, near):
        copies = []
        for t in range(1, wide_x * lanes):
            peer = near_at(t)
            copy = remote(part.at[lax.rem(peer[1], 2)], near.at[t], n_s.at[n, t], n_r.at[n, t], peer)
            copy.start()
            copies.append(copy)
        return copies

    def far_start(n, part, near, summed, far, copies):
        for copy in copies:
            copy.wait()
        total = part[core]
        for t in range(1, wide_x * lanes):
            total = total + near[t]
        summed[...] = total
        copies = []
        for t in range(1, deep_z):
            copy = remote(summed, far.at[t], z_s.at[n, t], z_r.at[n, t], far_at(t))
            copy.start()
            copies.append(copy)
        return copies

    def twin_start(n, summed, far, tot, copies):
        for copy in copies:
            copy.wait()
        total = summed[...]
        for t in range(1, deep_z):
            total = total + far[t]
        tot[core] = total
        copy = remote(tot.at[core], tot.at[core], t_s.at[n], t_r.at[n], (g, sibling))
        copy.start()
        return copy

    def relay(h):
        copies = [remote(gat.at[h, 0], gat.at[h, half], f_s.at[h, 0], f_r.at[h, 0], (g, sibling))]
        copies += [
            remote(gat.at[h, 0], gat.at[h, t], x_s.at[h, t], x_r.at[h, t], lane_at(2 * t))
            for t in range(1, half)
        ]
        for copy in copies:
            copy.start()
        return copies

    def pass_on(h, copies):
        passed = [copies[0]]
        for t in range(1, half):
            copies[t].wait()
            copy = remote(gat.at[h, t], gat.at[h, half + t], f_s.at[h, t], f_r.at[h, t], (g, sibling))
            copy.start()
            passed.append(copy)
        return passed

    half_lower = lax.broadcasted_iota(jnp.int32, (256, width), 1) < cut

    def widen(slot):
        def step(c, _):
            at = pl.multiple_of(c * 256, 256)
            first = gat[0, slot, pl.ds(at, 256)].astype(F32)
            second = gat[1, slot, pl.ds(at, 256)].astype(F32)
            wide[pl.ds(slot * rows + at, 256)] = jnp.where(half_lower, first, turn(second))
            wide[pl.ds(slot * rows + rows // 2 + at, 256)] = jnp.where(half_lower, turn(first), second)
            return 0

        lax.fori_loop(0, rows // 512, step, 0, unroll=2)

    halo_copies = [halo(0, 0), halo(0, 1)]
    small[2].wait()
    small[3].wait()
    codes[0] = dest_lane[...] * rows + dest_slot[...]
    code_copies = []
    for t in range(1, lanes):
        copy = remote(codes.at[0], codes.at[t], code_s.at[t], code_r.at[t], lane_at(t))
        copy.start()
        code_copies.append(copy)
    load_tiles.wait()
    for copy in small[4:]:
        copy.wait()

    relayed, near_copies = [None, None], [None, None]
    for k in range(1, ORDER + 1):
        for h in range(2):
            for copy in halo_copies[h]:
                copy.wait()
            unpack(k - 1, h)
            if k < ORDER:
                for b in (*range(quads), *range(2 * quads, 3 * quads)):
                    first = block(k, h, b)
                    keep_fields(h, b, first, block(k, h, b + quads))
                halo_copies[h] = halo(k, h)
            else:
                for b in range(own_blocks // 2):
                    first = block(k, h, b)
                    gat[h, 0, pl.ds(b * tile, tile)] = merge(
                        h, first, block(k, h, b + own_blocks // 2)
                    ).astype(BF)
                if h == 0:
                    own_gram = square()
                    head, tail = own_gram[: cut // 2], own_gram[cut // 2 : cut]
                    flat = lax.broadcasted_iota(jnp.int32, (cut // 2, width), 1) < cut
                    packed = jnp.where(flat, head, turn(tail))
                    for i in range(2):
                        part_a[i] = packed[i * cut // 4 : (i + 1) * cut // 4]
                    near_copies[0] = near_start(0, part_a, near_a)
                else:
                    own_gram = square()
                    for i in range(2):
                        part_b[i] = own_gram[cut + i * cut // 2 : cut + (i + 1) * cut // 2]
                    near_copies[1] = near_start(1, part_b, near_b)
                relayed[h] = relay(h)
        if k == 1:
            for copy in code_copies:
                copy.wait()
            source_copy = invert()

    far_copies_a = far_start(0, part_a, near_a, sum_a, far_a, near_copies[0])
    far_copies_b = far_start(1, part_b, near_b, sum_b, far_b, near_copies[1])
    passed_a = pass_on(0, relayed[0])
    twin_start(0, sum_a, far_a, tot_a, far_copies_a).wait()
    packed = jnp.concatenate([tot_a[0], tot_a[1]], axis=0)
    flat = lax.broadcasted_iota(jnp.int32, (cut // 2, width), 1) < cut
    corner = jnp.concatenate([jnp.where(flat, packed, 0.0), jnp.where(flat, turn(packed), 0.0)], axis=0)
    first_rows = eliminate(corner, 0, root)
    corner_inverse = exact_dot(first_rows, first_rows, 0, 0) * (1.0 / (root * root))
    passed_b = pass_on(1, relayed[1])
    for copy in (passed_a[0], passed_b[0]):
        copy.wait()
    widen(0)
    widen(half)
    twin = twin_start(1, sum_b, far_b, tot_b, far_copies_b)
    twin.wait()
    strip = jnp.concatenate([tot_b[0], tot_b[1]], axis=0)
    scaled = exact_dot(strip, corner_inverse, 1, 0)
    strip_square = jnp.concatenate([jnp.zeros((cut, width), F32), strip], axis=0)
    taken = exact_dot(scaled, strip_square, 1, 1)
    flat = lax.broadcasted_iota(jnp.int32, (cut, width), 1) < cut
    second_rows = eliminate(jnp.where(flat, -scaled, strip - taken), cut, root)
    whitener = jnp.concatenate([first_rows, second_rows], axis=0)
    top = whitener.astype(BF)
    rhs = jnp.concatenate([top, (whitener - top.astype(F32)).astype(BF)], axis=0)

    for t in range(1, half):
        for copy in (passed_a[t], passed_b[t]):
            copy.wait()
        widen(t)
        widen(half + t)
    source_copy.wait()

    radius = math.sqrt(width)
    ones = jnp.ones((2 * width, width), BF)

    def ball(c, _):
        at = pl.ds(pl.multiple_of(c * 256, 256), 256)
        picked = [wide[pl.ds(source_s[2 * c + r // tile, r % tile], 1), :] for r in range(256)]
        pair = lax.dot_general(
            jnp.concatenate(picked, axis=0).astype(BF), rhs, (((1,), (1,)), ((), ())), preferred_element_type=F32
        )
        white = pair[:, :width] + pair[:, width:]
        each = white * white
        head = each.astype(BF)
        parts = jnp.concatenate([head, (each - head.astype(F32)).astype(BF)], axis=1)
        squares = jnp.dot(parts, ones, preferred_element_type=F32) + 1e-06
        shrink = lax.rsqrt(squares)
        out[at] = (white * (jnp.tanh(squares * shrink / radius) * radius * shrink)).astype(BF)
        return 0

    lax.fori_loop(0, rows // 256, ball, 0, unroll=4)


def body(features, tiles, tile_cols, send_index, send_count, coef, dest_lane, dest_slot):
    groups, lanes = lax.axis_size("grp"), lax.axis_size("lane")
    rows, width = features.shape
    blocks, per_block, tile, _ = tiles.shape
    bnd = send_index.shape[2]
    half = lanes // 2
    wide_x = 1 << ((groups.bit_length() - 1) // 2)
    near, far = wide_x * lanes, groups // wide_x
    cut = width // 2
    whole_ext = pltpu.VMEM(((rows + 2 * bnd) // tile, tile, width), BF)
    dma = pltpu.SemaphoreType.DMA
    vmem = pl.BlockSpec(memory_space=pltpu.VMEM)
    hbm = pl.BlockSpec(memory_space=pltpu.HBM)
    return pl.pallas_call(
        functools.partial(kernel, groups, lanes, wide_x),
        out_shape=pltpu.VMEM((rows, width), BF),
        in_specs=[hbm] * 8,
        out_specs=vmem,
        scratch_shapes=[
            pltpu.SMEM((per_block, blocks), jnp.int32),
            pltpu.SMEM((1, 2), jnp.int32),
            pltpu.VMEM((2, bnd), jnp.int32),
            pltpu.VMEM((ORDER + 1, width), F32),
            pltpu.VMEM((rows // 128, 128), jnp.int32),
            pltpu.VMEM((rows // 128, 128), jnp.int32),
            pltpu.VMEM((rows // 128, 128), jnp.int32),
            pltpu.SMEM((rows // 128, 128), jnp.int32),
            *[whole_ext] * (2 * ORDER),
            pltpu.VMEM((blocks, per_block, tile, tile), BF),
            pltpu.VMEM((2 * bnd, rows // 4), BF),
            pltpu.VMEM((2 * bnd, width), jnp.int32),
            pltpu.VMEM((2, rows // 4, 2 * width), BF),
            pltpu.VMEM((ORDER, 2, bnd // tile, tile, width), BF),
            pltpu.VMEM((2, rows, width), F32),
            pltpu.VMEM((rows, width), BF),
            pltpu.VMEM((rows, width), BF),
            pltpu.VMEM((2, lanes, rows // 2, width), BF),
            pltpu.VMEM((lanes, rows // 128, 128), jnp.int32),
            pltpu.VMEM((2, cut // 4, width), F32),
            pltpu.VMEM((2, cut // 2, width), F32),
            pltpu.VMEM((near, cut // 4, width), F32),
            pltpu.VMEM((near, cut // 2, width), F32),
            pltpu.VMEM((cut // 4, width), F32),
            pltpu.VMEM((cut // 2, width), F32),
            pltpu.VMEM((far, cut // 4, width), F32),
            pltpu.VMEM((far, cut // 2, width), F32),
            pltpu.VMEM((2, cut // 4, width), F32),
            pltpu.VMEM((2, cut // 2, width), F32),
            pltpu.VMEM((lanes * rows, width), F32),
            dma((10,)),
            dma((ORDER, 2, 2)), dma((ORDER, 2, 2)),
            dma((lanes,)), dma((lanes,)),
            dma((2, near)), dma((2, near)),
            dma((2, far)), dma((2, far)),
            dma((2,)), dma((2,)),
            dma((2, half)), dma((2, half)),
            dma((2, half)), dma((2, half)),
        ],
        compiler_params=pltpu.CompilerParams(
            collective_id=0, has_side_effects=True, vmem_limit_bytes=61 * 1024 * 1024
        ),
    )(
        tile_cols.T, send_count, features.reshape(-1, tile, width), tiles, send_index.reshape(2, bnd), coef,
        dest_lane.reshape(-1, 128), dest_slot.reshape(-1, 128),
    )


def solution(mesh):
    placed = (
        P(("grp", "lane"), None),
        P(("grp", "lane"), None, None, None),
        P(("grp", "lane"), None),
        P(("grp", "lane"), None, None),
        P(("grp", "lane"), None),
        P(),
        P(("grp", "lane")),
        P(("grp", "lane")),
    )
    return jax.shard_map(
        body, mesh=mesh, in_specs=placed, out_specs=P(("grp", "lane"), None), check_vma=False
    )
```
